512 devices in a mesh: gx: 16 (over y, z_hi), gy: 32 (over z_lo, x, core).
Axes of the slice: x: 4, y: 4, z: 16 (z_hi: 4, z_lo: 4; z = z_hi * 4 + z_lo), core: 2. Of those that a mesh axis runs over, the one named last changes fastest.
Arguments:
- positions: float32 [16, 32, 3, 128], P('gx', 'gy'), may hold values from 0 to 24, as said below
- features: bfloat16 [16, 32, 128, 128], P('gx', 'gy'), may hold values from -6 to 6
- counts: int32 [16, 32], P('gx', 'gy'), may hold values from 16 to 128, as said below
- teacher: float32 [16, 32, 3, 128], P('gx', 'gy'), may hold values from -12 to 12
- confidence: float32 [16, 32, 128], P('gx', 'gy'), may hold values from 0.1 to 1
- radial_weights: float32 [8, 128], replicated, may hold values from -0.9 to 0.9
- square_coef: float32 [128], replicated, may hold values from 0.2 to 2
- linear_coef: float32 [128], replicated, may hold values from -4 to 4
Outputs:
- forces: float32 [16, 32, 3, 128], P('gx', 'gy')
- loss: float32 [], replicated
- grad_radial: float32 [8, 128], replicated
- grad_square: float32 [128], replicated
- grad_linear: float32 [128], replicated
The draws below stay inside these ranges and needn't reach their ends.
Inputs may be any that keep to these rules, and one draw needn't show every extreme that they name: Cell (p,q) holds atoms in its first counts[p,q] slots; some cell is full and some holds 16 atoms. `positions`: the first two coordinates lie in the cell's edge of 6, the third in a film 24 thick.
All inputs are finite; a program needn't handle non-finite values.
Results may differ from the reference program's by a relative error of at most 0.006.
Values may be sent and summed in bfloat16 or wider, within the bound.
A program may use at most 64 MiB of HBM per device.

```python
import math
import jax
import jax.numpy as jnp
from jax import lax

C = 128
NB = 8
ATOMS = 128
CELLS_X = 16
CELLS_Y = 32


def draw_positions(key, part):
    unit = jax.random.uniform(key, (CELLS_X, CELLS_Y, 3, ATOMS), jnp.float32)
    extent = jnp.array([6.0, 6.0, 24.0], jnp.float32)[None, None, :, None]
    return unit * extent


def draw_counts(key, part):
    cell_total = CELLS_X * CELLS_Y
    counts_flat = jax.random.randint(key, (cell_total,), ATOMS // 8, ATOMS + 1)
    top_cell = jax.random.randint(jax.random.fold_in(key, 11), (), 0, cell_total)
    low_cell = (top_cell + 1 + jax.random.randint(jax.random.fold_in(key, 12), (), 0, cell_total - 1)) % cell_total
    counts_flat = counts_flat.at[top_cell].set(ATOMS).at[low_cell].set(ATOMS // 8)
    return counts_flat.reshape(CELLS_X, CELLS_Y).astype(jnp.int32)


def block_scale(rng, shape, cuts, least, largest):
    def one(axis_at, shards_of):
        draws = jax.random.uniform(jax.random.fold_in(jax.random.fold_in(rng, 6), axis_at), (shards_of,), jnp.float32, least / len(cuts), largest / len(cuts))
        return jnp.repeat(jnp.exp(draws), shape[axis_at] // shards_of).reshape((-1,) + (1,) * (len(shape) - axis_at - 1))

    gain = one(*cuts[0])
    for cut in cuts[1:]:
        gain = gain * one(*cut)
    return gain


def scatter_about(rng, dims, scale, bound, cuts=(), kind=jnp.bfloat16):
    values = jax.random.normal(rng, dims, jnp.float32) * scale
    if len(cuts) > 0:
        values = block_scale(rng, dims, cuts, -0.22, 0.18) * values
    return jnp.clip(values, min=-bound, max=bound).astype(kind)


def setup_inputs(seed: int = 0) -> dict:
    key_list = jax.random.split(jax.random.key(seed), 9)
    return {
        "positions": draw_positions(jax.random.fold_in(key_list[8], 71), 0),
        "features": scatter_about(key_list[1], (CELLS_X, CELLS_Y, ATOMS, C), 1.0, 6.0, ((0, 16), (1, 32))),
        "counts": draw_counts(jax.random.fold_in(key_list[8], 71), 0),
        "teacher": scatter_about(key_list[3], (CELLS_X, CELLS_Y, 3, ATOMS), 2.0, 12.0, ((0, 16), (1, 32)), jnp.float32),
        "confidence": jnp.clip(jnp.exp(math.log(1.0) - 2.3025851 * jax.random.uniform(key_list[4], (CELLS_X, CELLS_Y, ATOMS), jnp.float32) ** block_scale(key_list[4], (CELLS_X, CELLS_Y, ATOMS), ((0, 16), (1, 32)), -0.2, 0.2)), 0.1, 1.0),
        "radial_weights": scatter_about(key_list[5], (NB, C), 0.15, 0.9, (), jnp.float32),
        "square_coef": jnp.clip(jnp.exp(jax.random.uniform(key_list[6], (C,), jnp.float32, math.log(0.2), math.log(2.0))), 0.2, 2.0),
        "linear_coef": scatter_about(key_list[7], (C,), 1.0, 4.0, (), jnp.float32),
    }


CUTOFF = 6.0
CELL_EDGE = 6.0
SIGN_LIST = (1.0, -1.0, -1.0, -1.0)
HALF_SHELL = ((0, 0), (1, -1), (1, 0), (1, 1), (0, 1))
FULL_SHELL = ((0, 0), (-1, -1), (-1, 0), (-1, 1), (0, -1), (0, 1), (1, -1), (1, 0), (1, 1))


def contract(pattern, first_op, second_op):
    return jnp.einsum(pattern, first_op.astype(jnp.float32), second_op.astype(jnp.float32), precision=lax.Precision.HIGHEST)


def decay_rates(basis):
    return 0.5 * jnp.power(1.6, jnp.arange(basis, dtype=jnp.float32))


def tile_geometry(own_pos, own_mask, part_pos, part_mask, off_x, off_y, basis):
    offset_vec = jnp.array([off_x * CELL_EDGE, off_y * CELL_EDGE, 0.0], jnp.float32)
    displace = part_pos[:, :, None, :] + offset_vec[None, :, None, None] - own_pos[:, :, :, None]
    scaled = jnp.sum(displace * displace, axis=1) / (CUTOFF * CUTOFF)
    paired = own_mask[:, :, None] * part_mask[:, None, :]
    if off_x == 0 and off_y == 0:
        slot_count = own_pos.shape[-1]
        paired = paired * (1.0 - jnp.eye(slot_count, dtype=jnp.float32))[None]
    margin = jnp.maximum(1.0 - scaled, 0.0)
    smooth = margin * margin * margin * paired
    smooth_slope = -3.0 * margin * margin * paired
    rates = decay_rates(basis)[None, :, None, None]
    decays = jnp.exp(-rates * scaled[:, None])
    radial = decays * smooth[:, None]
    radial_slope = decays * (smooth_slope[:, None] - rates * smooth[:, None])
    angular = jnp.concatenate([jnp.ones_like(scaled)[:, None], displace / CUTOFF], axis=1)
    return displace, radial, radial_slope, angular


def kernel_of(geometry):
    displace, radial, radial_slope, angular = geometry
    return (radial[:, :, None] * angular[:, None]).astype(jnp.bfloat16)


def tangent_of(geometry, own_dir, part_dir):
    displace, radial, radial_slope, angular = geometry
    rate_diff = part_dir[:, :, None, :] - own_dir[:, :, :, None]
    scaled_rate = 2.0 * jnp.sum(displace * rate_diff, axis=1) / (CUTOFF * CUTOFF)
    angular_rate = jnp.concatenate([jnp.zeros_like(scaled_rate)[:, None], rate_diff / CUTOFF], axis=1)
    moved = (radial_slope * scaled_rate[:, None])[:, :, None] * angular[:, None] + radial[:, :, None] * angular_rate[:, None]
    return moved.astype(jnp.bfloat16)


def pair_gradient(cotangent, geometry):
    displace, radial, radial_slope, angular = geometry
    radial_part = jnp.sum(cotangent * angular[:, None], axis=2)
    angular_part = jnp.sum(cotangent * radial[:, :, None], axis=1)
    scaled_part = jnp.sum(radial_part * radial_slope, axis=1)
    return scaled_part[:, None] * (2.0 / (CUTOFF * CUTOFF)) * displace + angular_part[:, 1:] / CUTOFF


def channel_mix(feature_rows, radial_weights):
    return (feature_rows.astype(jnp.float32)[:, None] * radial_weights[None, :, None, :]).astype(jnp.bfloat16)


def reference(positions, features, counts, teacher, confidence, radial_weights, square_coef, linear_coef):
    cells_x, cells_y = counts.shape
    slot_count = positions.shape[-1]
    channels = features.shape[-1]
    basis = radial_weights.shape[0]
    cell_count = cells_x * cells_y
    atom_total = float(cell_count * slot_count)
    atom_mask = (jnp.arange(slot_count, dtype=jnp.int32)[None, None, :] < counts[:, :, None]).astype(jnp.float32)
    sign_vec = jnp.array(SIGN_LIST, jnp.float32).astype(jnp.bfloat16)[None, :, None, None]
    linear_row = jnp.broadcast_to(linear_coef.astype(jnp.bfloat16)[None, None, None, :], (1, 1, slot_count, channels))
    zero_row = jnp.zeros((1, 1, slot_count, channels), jnp.bfloat16)

    def pick(grid_vals, cell_index, off_x, off_y):
        row_index = ((cell_index // cells_y + off_x) % cells_x).astype(jnp.int32)
        col_index = ((cell_index % cells_y + off_y) % cells_y).astype(jnp.int32)
        return grid_vals[row_index, col_index][None]

    def geometry_at(cell_index, off_x, off_y):
        return tile_geometry(pick(positions, cell_index, 0, 0), pick(atom_mask, cell_index, 0, 0),
                             pick(positions, cell_index, off_x, off_y), pick(atom_mask, cell_index, off_x, off_y),
                             off_x, off_y, basis)

    def per_cell(function):
        group_size = math.gcd(cell_count, 16)
        ids = jnp.arange(cell_count, dtype=jnp.int32).reshape(-1, group_size)
        outcome = lax.map(jax.vmap(function), ids)
        return jax.tree.map(lambda element: element.reshape((cell_count,) + element.shape[2:]), outcome)

    def value_cell(cell_index):
        totals = jnp.zeros((1, 4, slot_count, channels), jnp.float32)
        for off_x, off_y in FULL_SHELL:
            kernel = kernel_of(geometry_at(cell_index, off_x, off_y))
            part_mix = channel_mix(pick(features, cell_index, off_x, off_y), radial_weights)
            totals = totals + contract("nkaij,nkjc->naic", kernel, part_mix)
        return totals[0, 1:]

    vectors = per_cell(value_cell).reshape(cells_x, cells_y, 3, slot_count, channels)
    cot_grid = (2.0 * square_coef * vectors).astype(jnp.bfloat16)

    def full_cot(cell_index, off_x, off_y):
        return jnp.concatenate([linear_row, pick(cot_grid, cell_index, off_x, off_y)], axis=1)

    def force_cell(cell_index):
        own_mix = channel_mix(pick(features, cell_index, 0, 0), radial_weights)
        own_cot = full_cot(cell_index, 0, 0)
        own_force = jnp.zeros((1, 3, slot_count), jnp.float32)
        backs = []
        for off_x, off_y in HALF_SHELL:
            geometry = geometry_at(cell_index, off_x, off_y)
            part_mix = channel_mix(pick(features, cell_index, off_x, off_y), radial_weights)
            cotangent = contract("naic,nkjc->nkaij", own_cot, part_mix)
            selfpair = off_x == 0 and off_y == 0
            if not selfpair:
                cotangent = cotangent + contract("nkic,najc->nkaij", own_mix, full_cot(cell_index, off_x, off_y) * sign_vec)
            pull = pair_gradient(cotangent, geometry)
            own_force = own_force + jnp.sum(pull, axis=3)
            if selfpair:
                own_force = own_force - jnp.sum(pull, axis=2)
            else:
                backs.append(-jnp.sum(pull, axis=2)[0])
        return own_force[0], jnp.stack(backs)

    own_force, backs = per_cell(force_cell)
    forces = own_force.reshape(cells_x, cells_y, 3, slot_count)
    for number, (off_x, off_y) in enumerate(HALF_SHELL[1:]):
        forces = forces + jnp.roll(backs[:, number].reshape(cells_x, cells_y, 3, slot_count), (off_x, off_y), axis=(0, 1))
    weights = confidence * atom_mask
    difference = forces - teacher
    loss = jnp.sum(weights[:, :, None] * difference * difference) / atom_total
    delta = -2.0 * weights[:, :, None] * difference / atom_total

    def tangent_cell(cell_index):
        totals = jnp.zeros((1, 4, slot_count, channels), jnp.float32)
        own_dir = pick(delta, cell_index, 0, 0)
        for off_x, off_y in FULL_SHELL:
            moved = tangent_of(geometry_at(cell_index, off_x, off_y), own_dir, pick(delta, cell_index, off_x, off_y))
            part_mix = channel_mix(pick(features, cell_index, off_x, off_y), radial_weights)
            totals = totals + contract("nkaij,nkjc->naic", moved, part_mix)
        return totals[0]

    rates_all = per_cell(tangent_cell)
    grad_linear = jnp.sum(rates_all[:, 0], axis=(0, 1))
    rates = rates_all[:, 1:].reshape(cells_x, cells_y, 3, slot_count, channels)
    grad_square = jnp.sum(2.0 * vectors * rates, axis=(0, 1, 2, 3))
    adjoint_grid = (2.0 * square_coef * rates).astype(jnp.bfloat16)

    def weight_cell(cell_index):
        own_adj = jnp.concatenate([zero_row, pick(adjoint_grid, cell_index, 0, 0)], axis=1)
        own_cot = full_cot(cell_index, 0, 0)
        own_dir = pick(delta, cell_index, 0, 0)
        grad_w = jnp.zeros((basis, channels), jnp.float32)
        for off_x, off_y in FULL_SHELL:
            geometry = geometry_at(cell_index, off_x, off_y)
            kernel = kernel_of(geometry)
            moved = tangent_of(geometry, own_dir, pick(delta, cell_index, off_x, off_y))
            part_feat = pick(features, cell_index, off_x, off_y)
            weight_side = contract("nkaij,naic->nkjc", kernel, own_adj) + contract("nkaij,naic->nkjc", moved, own_cot)
            grad_w = grad_w + jnp.sum(part_feat.astype(jnp.float32)[:, None] * weight_side, axis=(0, 2))
        return grad_w

    grad_radial = jnp.sum(per_cell(weight_cell), axis=0)
    return forces, loss, grad_radial, grad_square, grad_linear
```

```python
import functools

import numpy as np
import jax
import jax.numpy as jnp
from jax import lax
from jax.experimental import pallas as pl
from jax.experimental.pallas import tpu as pltpu
from jax.sharding import PartitionSpec as P

EDGE = 6.0
MESH = pl.DeviceIdType.MESH
F32 = jnp.float32
BF16 = jnp.bfloat16
N = 128
NB = 8
TILES = 9
CENTER = 4
ROWS = 32
CHUNKS = N // ROWS
RATES = [float(np.float32(0.5) * np.float32(1.6) ** np.float32(k)) for k in range(NB)]
G_ROWS = 16


def shift_of(tile):
    return tile // 3 - 1, tile % 3 - 1


def groups_of(nx, ny):
    inner_y = min(8, ny)
    inner_x = min(4, nx)
    groups = [("gy", 1, inner_y), ("gx", inner_x, nx // inner_x), ("gy", inner_y, ny // inner_y), ("gx", 1, inner_x)]
    return [g for g in groups if g[2] > 1]


def fold(values):
    rows, cols = values.shape
    return jnp.sum(values.reshape(rows // 8, 8, cols), axis=0)


def split_rows(values):
    high = values.astype(BF16)
    low = (values - high.astype(F32)).astype(BF16)
    return high, low


def kernel(
    nx, ny, pos_ref, feat_ref, count_ref, teach_ref, conf_ref, w_ref, sq_ref, lin_ref,
    force_ref, loss_ref, gw_ref, gsq_ref, glin_ref,
    pack, fe, own_pos, phi, phis, kb, ak, vv, cw, ps, lj, pf, back, back_in, delta, own_dir, sp, rt, gp, *rest,
):
    groups = groups_of(nx, ny)
    ar_bufs = rest[: len(groups)]
    send_pos, recv_pos, send_feat, recv_feat, send_back, recv_back, send_delta, recv_delta, send_ar, recv_ar = rest[len(groups):]
    my_x = lax.axis_index("gx")
    my_y = lax.axis_index("gy")

    def neighbour(tile):
        off_x, off_y = shift_of(tile)
        return (lax.rem(my_x + off_x + nx, nx), lax.rem(my_y + off_y + ny, ny))

    def member(group, step):
        axis, stride, size = group
        base = my_x if axis == "gx" else my_y
        place = lax.rem(base // stride, size)
        other = base + (lax.rem(place + step, size) - place) * stride
        return place, ((other, my_y) if axis == "gx" else (my_x, other))

    around = [t for t in range(TILES) if t != CENTER]
    barrier = pltpu.get_barrier_semaphore()
    signals = 0
    for tile in around:
        pl.semaphore_signal(barrier, inc=1, device_id=neighbour(tile), device_id_type=MESH)
        signals += 1
    for group in groups:
        for step in range(1, group[2]):
            pl.semaphore_signal(barrier, inc=1, device_id=member(group, step)[1], device_id_type=MESH)
            signals += 1

    mask = (lax.broadcasted_iota(jnp.int32, (1, N), 1) < count_ref[...]).astype(F32)
    pack[CENTER, 0:3] = pos_ref[...]
    pack[CENTER, 3:4] = mask
    for b in range(3):
        own_pos[b] = jnp.transpose(jnp.broadcast_to(pos_ref[b : b + 1, :], (N, N)))
    own_pos[3] = jnp.transpose(jnp.broadcast_to(mask, (N, N)))
    fe[CENTER * N : (CENTER + 1) * N, :] = feat_ref[...]
    pf[...] = jnp.zeros_like(pf)
    back[...] = jnp.zeros_like(back)
    delta[CENTER] = jnp.zeros((4, N), F32)
    sp[...] = jnp.zeros_like(sp)
    vv[...] = jnp.zeros_like(vv)
    rt[...] = jnp.zeros_like(rt)
    pl.semaphore_wait(barrier, signals)

    def send_pack(tile):
        slot = TILES - 1 - tile
        return pltpu.make_async_remote_copy(
            src_ref=pack.at[CENTER], dst_ref=pack.at[slot], send_sem=send_pos.at[slot], recv_sem=recv_pos.at[slot],
            device_id=neighbour(tile), device_id_type=MESH)

    def send_features(source, tile, slot):
        block = feat_ref if source == CENTER else fe.at[pl.ds(source * N, N), :]
        return pltpu.make_async_remote_copy(
            src_ref=block, dst_ref=fe.at[pl.ds(slot * N, N), :], send_sem=send_feat.at[slot], recv_sem=recv_feat.at[slot],
            device_id=neighbour(tile), device_id_type=MESH)

    pack_copies = {t: send_pack(t) for t in around}
    for t in (0, 1, 2, 6, 7, 8, 3, 5):
        pack_copies[t].start()
    feat_copies = {7: send_features(CENTER, 1, 7), 1: send_features(CENTER, 7, 1),
                   5: send_features(CENTER, 3, 5), 3: send_features(CENTER, 5, 3)}
    for t in (7, 1, 5, 3):
        feat_copies[t].start()

    def geometry(tile, rows):
        off_x = ((tile // 3 - 1) * 6).astype(F32)
        off_y = ((lax.rem(tile, 3) - 1) * 6).astype(F32)
        part = pack[tile]
        disp = [
            (part[0:1] + off_x) - own_pos[0, rows, :],
            (part[1:2] + off_y) - own_pos[1, rows, :],
            part[2:3] - own_pos[2, rows, :],
        ]
        return part, disp

    def shape_tile(step, carry):
        tile = lax.rem(step // CHUNKS + CENTER, TILES)
        chunk = lax.rem(step, CHUNKS)

        @pl.when((chunk == 0) & (step >= CHUNKS))
        def _():
            pltpu.make_async_remote_copy(
                src_ref=pack.at[CENTER], dst_ref=pack.at[tile], send_sem=send_pos.at[tile], recv_sem=recv_pos.at[tile],
                device_id=neighbour(0), device_id_type=MESH).wait_recv()

        start = pl.multiple_of(chunk * ROWS, ROWS)
        rows = pl.ds(start, ROWS)
        cols = pl.ds(pl.multiple_of(tile * N, N), N)
        part, disp = geometry(tile, rows)
        scaled = (disp[0] * disp[0] + disp[1] * disp[1] + disp[2] * disp[2]) * (1.0 / 36.0)
        same = (lax.broadcasted_iota(jnp.int32, (ROWS, N), 0) + start) == lax.broadcasted_iota(jnp.int32, (ROWS, N), 1)
        centred = jnp.where(tile == CENTER, 1.0, 0.0)
        paired = own_pos[3, rows, :] * part[3:4] * (1.0 - jnp.where(same, 1.0, 0.0) * centred)
        margin = jnp.maximum(1.0 - scaled, 0.0)
        square = margin * margin * paired
        smooth = margin * square
        slope = -3.0 * square
        ang = [disp[b] * (1.0 / 6.0) for b in range(3)]
        for k in range(NB):
            decay = jnp.exp(scaled * (-RATES[k]))
            radial = decay * smooth
            phi[tile * NB + k, rows, :] = radial
            phis[tile * NB + k, rows, :] = decay * (slope - RATES[k] * smooth)
            for b in range(3):
                line = pl.ds(pl.multiple_of((k * 3 + b) * N + start, ROWS), ROWS)
                kb[line, cols] = (radial * ang[b]).astype(BF16)
        return carry

    lax.fori_loop(0, TILES * CHUNKS, shape_tile, 0)

    feat_copies[7].wait_recv()
    feat_copies[1].wait_recv()
    for source, tile in ((1, 3), (7, 3), (1, 5), (7, 5)):
        slot = source + (1 if tile == 3 else -1)
        feat_copies[slot] = send_features(source, tile, slot)
        feat_copies[slot].start()
    for slot in (3, 5, 0, 2, 6, 8):
        feat_copies[slot].wait_recv()

    lin_row = lin_ref[...].astype(BF16).astype(F32)
    high, low = split_rows(w_ref[...] * lin_row)
    pair_dims = (((1,), (1,)), ((), ()))
    for t in range(TILES):
        block = fe[t * N : (t + 1) * N, :]
        lj[t] = lax.dot_general(high, block, pair_dims, preferred_element_type=F32) + lax.dot_general(
            low, block, pair_dims, preferred_element_type=F32)

    def gather_vectors(half, carry):
        first = pl.multiple_of(half * 768, 768)
        sums = jnp.dot(kb[pl.ds(first, 768), :], fe[...], preferred_element_type=F32)
        ak[pl.ds(first, 768), :] = sums
        vv[...] += sums[:384] * w_ref[pl.ds(half * 2, 1), :] + sums[384:] * w_ref[pl.ds(half * 2 + 1, 1), :]
        return carry

    lax.fori_loop(0, NB // 2, gather_vectors, 0)
    twice = 2.0 * sq_ref[...]
    for k in range(NB):
        cw[k * 384 : (k + 1) * 384, :] = (vv[...] * (twice * w_ref[k : k + 1, :])).astype(BF16)

    def send_back_row(tile):
        return pltpu.make_async_remote_copy(
            src_ref=back.at[tile], dst_ref=back_in.at[tile], send_sem=send_back.at[tile], recv_sem=recv_back.at[tile],
            device_id=neighbour(tile), device_id_type=MESH)

    def pull_tile(step, carry):
        tile = lax.rem(step + 6, TILES)
        block = fe[pl.ds(pl.multiple_of(tile * N, N), N), :]
        ps[...] = lax.dot_general(cw[...], block, pair_dims, preferred_element_type=F32)
        level = lj[tile]

        def pull_rows(chunk, totals):
            start = pl.multiple_of(chunk * ROWS, ROWS)
            rows = pl.ds(start, ROWS)
            part, disp = geometry(tile, rows)
            ang = [disp[b] * (1.0 / 6.0) for b in range(3)]
            along = jnp.zeros((ROWS, N), F32)
            across = [jnp.zeros((ROWS, N), F32) for _ in range(3)]
            for k in range(NB):
                radial = phi[tile * NB + k, rows, :]
                inner = level[k : k + 1, :]
                for b in range(3):
                    pair = ps[pl.ds(pl.multiple_of((k * 3 + b) * N + start, ROWS), ROWS), :]
                    inner = inner + ang[b] * pair
                    across[b] = across[b] + radial * pair
                along = along + phis[tile * NB + k, rows, :] * inner
            along = along * (1.0 / 3.0)
            sums = []
            for b in range(3):
                pull = along * ang[b] + across[b] * (1.0 / 6.0)
                pf[b, rows, :] += pull
                sums.append(totals[b] + fold(pull))
            return tuple(sums)

        zero = jnp.zeros((8, N), F32)
        totals = lax.fori_loop(0, CHUNKS, pull_rows, (zero, zero, zero))
        for b in range(3):
            back[tile, b : b + 1] = jnp.sum(totals[b], axis=0, keepdims=True)

        @pl.when(tile != CENTER)
        def _():
            send_back_row(tile).start()

        return carry

    lax.fori_loop(0, TILES, pull_tile, 0)
    forces = jnp.concatenate(
        [jnp.sum(jnp.transpose(pf[b]), axis=0, keepdims=True) for b in range(3)], axis=0) - back[CENTER, 0:3]
    for tile in around:
        send_back_row(tile).wait_recv()
        forces = forces - back_in[tile, 0:3]
    weights = conf_ref[...] * mask
    difference = forces - teach_ref[...]
    atom_total = 1.0 / float(nx * ny * N)
    force_ref[...] = forces
    loss_row = jnp.sum(weights * difference * difference, axis=0, keepdims=True) * atom_total
    delta[CENTER, 0:3] = (-2.0 * atom_total) * weights * difference

    def send_error(tile):
        slot = TILES - 1 - tile
        return pltpu.make_async_remote_copy(
            src_ref=delta.at[CENTER], dst_ref=delta.at[slot], send_sem=send_delta.at[slot], recv_sem=recv_delta.at[slot],
            device_id=neighbour(tile), device_id_type=MESH)

    for t in (0, 1, 2, 6, 7, 8, 3, 5):
        send_error(t).start()
    for b in range(3):
        own_dir[b] = jnp.transpose(jnp.broadcast_to(delta[CENTER, b : b + 1], (N, N)))

    def move_tile(step, carry):
        tile = lax.rem(step // CHUNKS + CENTER, TILES)
        chunk = lax.rem(step, CHUNKS)

        @pl.when((chunk == 0) & (step >= CHUNKS))
        def _():
            pltpu.make_async_remote_copy(
                src_ref=delta.at[CENTER], dst_ref=delta.at[tile], send_sem=send_delta.at[tile],
                recv_sem=recv_delta.at[tile], device_id=neighbour(0), device_id_type=MESH).wait_recv()

        start = pl.multiple_of(chunk * ROWS, ROWS)
        rows = pl.ds(start, ROWS)
        cols = pl.ds(pl.multiple_of(tile * N, N), N)
        part, disp = geometry(tile, rows)
        ang = [disp[b] * (1.0 / 6.0) for b in range(3)]
        errors = delta[tile]
        turn = [(errors[b : b + 1] - own_dir[b, rows, :]) * (1.0 / 6.0) for b in range(3)]
        scaled_rate = 2.0 * (ang[0] * turn[0] + ang[1] * turn[1] + ang[2] * turn[2])
        for k in range(NB):
            level = phis[tile * NB + k, rows, :] * scaled_rate
            radial = phi[tile * NB + k, rows, :]
            sp[tile * NB + k] += fold(level)
            for b in range(3):
                line = pl.ds(pl.multiple_of((k * 3 + b) * N + start, ROWS), ROWS)
                kb[line, cols] = (level * ang[b] + radial * turn[b]).astype(BF16)
        return carry

    lax.fori_loop(0, TILES * CHUNKS, move_tile, 0)

    def gather_rates(half, carry):
        first = pl.multiple_of(half * 768, 768)
        sums = jnp.dot(kb[pl.ds(first, 768), :], fe[...], preferred_element_type=F32)
        rt[...] += sums[:384] * w_ref[pl.ds(half * 2, 1), :] + sums[384:] * w_ref[pl.ds(half * 2 + 1, 1), :]
        gp[half * 2] = fold(sums[:384] * vv[...])
        gp[half * 2 + 1] = fold(sums[384:] * vv[...])
        return carry

    lax.fori_loop(0, NB // 2, gather_rates, 0)

    def weigh(k, carry):
        lines = pl.ds(pl.multiple_of(k * 384, 384), 384)
        gp[k] += fold(ak[lines, :] * rt[...])
        return carry

    lax.fori_loop(0, NB, weigh, 0)
    level_sum = jnp.zeros((NB, N), F32)
    for t in range(TILES):
        high, low = split_rows(jnp.sum(sp[t * NB : (t + 1) * NB], axis=1))
        block = fe[t * N : (t + 1) * N, :]
        level_sum = level_sum + jnp.dot(high, block, preferred_element_type=F32) + jnp.dot(
            low, block, preferred_element_type=F32)
    result = jnp.concatenate([
        jnp.sum(gp[...], axis=1) * twice + lin_row * level_sum,
        2.0 * jnp.sum(fold(vv[...] * rt[...]), axis=0, keepdims=True),
        jnp.sum(w_ref[...] * level_sum, axis=0, keepdims=True),
        loss_row,
        jnp.zeros((G_ROWS - NB - 3, N), F32),
    ], axis=0)

    number = 0
    for group, buf in zip(groups, ar_bufs):
        place = member(group, 0)[0]
        buf[place] = result
        copies = []
        for step in range(1, group[2]):
            copy = pltpu.make_async_remote_copy(
                src_ref=buf.at[place], dst_ref=buf.at[place], send_sem=send_ar.at[number], recv_sem=recv_ar.at[number],
                device_id=member(group, step)[1], device_id_type=MESH)
            number += 1
            copy.start()
            copies.append(copy)
        for copy in copies:
            copy.wait_recv()
        result = jnp.sum(buf[...], axis=0)
        for copy in copies:
            copy.wait_send()

    gw_ref[...] = result[0:NB]
    gsq_ref[...] = result[NB : NB + 1]
    glin_ref[...] = result[NB + 1 : NB + 2]
    loss_ref[...] = jnp.sum(result[NB + 2 : NB + 3], axis=1, keepdims=True)
    for tile in around:
        pack_copies[tile].wait_send()
        feat_copies[tile].wait_send()
        send_back_row(tile).wait_send()
        send_error(tile).wait_send()


def body(nx, ny, positions, features, counts, teacher, confidence, radial_weights, square_coef, linear_coef):
    groups = groups_of(nx, ny)
    copies = sum(g[2] - 1 for g in groups)
    vmem = pl.BlockSpec(memory_space=pltpu.VMEM)
    outs = pl.pallas_call(
        functools.partial(kernel, nx, ny),
        out_shape=(
            jax.ShapeDtypeStruct((3, N), F32),
            jax.ShapeDtypeStruct((1, 1), F32),
            jax.ShapeDtypeStruct((NB, N), F32),
            jax.ShapeDtypeStruct((1, N), F32),
            jax.ShapeDtypeStruct((1, N), F32),
        ),
        in_specs=[vmem] * 8,
        out_specs=(vmem,) * 5,
        scratch_shapes=[
            pltpu.VMEM((TILES, 4, N), F32),
            pltpu.VMEM((TILES * N, N), BF16),
            pltpu.VMEM((4, N, N), F32),
            pltpu.VMEM((TILES * NB, N, N), F32),
            pltpu.VMEM((TILES * NB, N, N), F32),
            pltpu.VMEM((3 * NB * N, TILES * N), BF16),
            pltpu.VMEM((3 * NB * N, N), F32),
            pltpu.VMEM((3 * N, N), F32),
            pltpu.VMEM((3 * NB * N, N), BF16),
            pltpu.VMEM((3 * NB * N, N), F32),
            pltpu.VMEM((TILES, NB, N), F32),
            pltpu.VMEM((3, N, N), F32),
            pltpu.VMEM((TILES, 4, N), F32),
            pltpu.VMEM((TILES, 4, N), F32),
            pltpu.VMEM((TILES, 4, N), F32),
            pltpu.VMEM((3, N, N), F32),
            pltpu.VMEM((TILES * NB, 8, N), F32),
            pltpu.VMEM((3 * N, N), F32),
            pltpu.VMEM((NB, 8, N), F32),
        ]
        + [pltpu.VMEM((g[2], G_ROWS, N), F32) for g in groups]
        + [pltpu.SemaphoreType.DMA((TILES,))] * 8
        + [pltpu.SemaphoreType.DMA((copies,))] * 2,
        compiler_params=pltpu.CompilerParams(
            collective_id=0, has_side_effects=True, vmem_limit_bytes=60 * 1024 * 1024),
        name="message_layer",
    )(
        positions.reshape(3, N), features.reshape(N, N), counts, teacher.reshape(3, N), confidence.reshape(1, N),
        radial_weights, square_coef.reshape(1, N), linear_coef.reshape(1, N),
    )
    forces, loss, grad_w, grad_sq, grad_lin = outs
    return (forces.reshape(1, 1, 3, N), loss.reshape(()), grad_w, grad_sq.reshape(N), grad_lin.reshape(N))


def solution(mesh):
    in_specs = (
        P("gx", "gy", None, None),
        P("gx", "gy", None, None),
        P("gx", "gy"),
        P("gx", "gy", None, None),
        P("gx", "gy", None),
        P(),
        P(),
        P(),
    )
    out_specs = (P("gx", "gy", None, None), P(), P(), P(), P())
    step = functools.partial(body, mesh.shape["gx"], mesh.shape["gy"])
    return jax.shard_map(step, mesh=mesh, in_specs=in_specs, out_specs=out_specs, check_vma=False)
```

```python
import functools

import numpy as np
import jax
import jax.numpy as jnp
from jax import lax
from jax.experimental import pallas as pl
from jax.experimental.pallas import tpu as pltpu
from jax.sharding import PartitionSpec as P

EDGE = 6.0
MESH = pl.DeviceIdType.MESH
F32 = jnp.float32
BF16 = jnp.bfloat16
N = 128
NB = 8
TILES = 9
CENTER = 4
ROWS = 32
CHUNKS = N // ROWS
RATES = [float(np.float32(0.5) * np.float32(1.6) ** np.float32(k)) for k in range(NB)]
G_ROWS = 12
ORDER = (4, 3, 5, 1, 7, 0, 2, 6, 8)
PLACE = tuple(ORDER.index(t) for t in range(TILES))
TABLE = sum(t * 9**p for p, t in enumerate(ORDER))


def shift_of(tile):
    return tile // 3 - 1, tile % 3 - 1


def groups_of(nx, ny):
    inner_y = min(8, ny)
    inner_x = min(4, nx)
    groups = [
        (("gy", 1, inner_y),),
        (("gx", inner_x, nx // inner_x), ("gy", inner_y, ny // inner_y)),
        (("gx", 1, inner_x),),
    ]
    return [g for g in groups if size_of(g) > 1]


def size_of(group):
    total = 1
    for part in group:
        total *= part[2]
    return total


def fold(values):
    rows, cols = values.shape
    return jnp.sum(values.reshape(rows // 8, 8, cols), axis=0)


def split_rows(values):
    high = values.astype(BF16)
    low = (values - high.astype(F32)).astype(BF16)
    return high, low


def kernel(
    nx, ny, pos_ref, feat_ref, count_ref, teach_ref, conf_ref, w_ref, sq_ref, lin_ref,
    force_ref, sum_ref,
    pack, fe, own_pos, phi, phis, kb, ak, vv, cw, ps, pf, back, back_in, delta, own_dir, sp, rt, gp, *rest,
):
    groups = groups_of(nx, ny)
    ar_bufs = rest[: len(groups)]
    send_pos, recv_pos, send_feat, recv_feat, send_back, recv_back, send_delta, recv_delta, send_ar, recv_ar = rest[len(groups):]
    my_x = lax.axis_index("gx")
    my_y = lax.axis_index("gy")

    def neighbour(tile):
        off_x, off_y = shift_of(tile)
        return (lax.rem(my_x + off_x + nx, nx), lax.rem(my_y + off_y + ny, ny))

    def member(group, step):
        place = 0
        target = {"gx": my_x, "gy": my_y}
        for axis, stride, size in reversed(group):
            base = target[axis]
            spot = lax.rem(base // stride, size)
            place = place * size + spot
            target[axis] = base + (lax.rem(spot + step % size, size) - spot) * stride
            step = step // size
        return place, (target["gx"], target["gy"])

    around = [t for t in range(TILES) if t != CENTER]
    barrier = pltpu.get_barrier_semaphore()
    signals = 0
    for tile in around:
        pl.semaphore_signal(barrier, inc=1, device_id=neighbour(tile), device_id_type=MESH)
        signals += 1
    for group in groups:
        for step in range(1, size_of(group)):
            pl.semaphore_signal(barrier, inc=1, device_id=member(group, step)[1], device_id_type=MESH)
            signals += 1

    mask = (lax.broadcasted_iota(jnp.int32, (1, N), 1) < count_ref[...]).astype(F32)
    for b in range(3):
        pack[CENTER, b : b + 1] = pos_ref[b]
    pack[CENTER, 3:4] = mask
    for b in range(3):
        own_pos[b] = jnp.transpose(jnp.broadcast_to(pos_ref[b], (N, N)))
    own_pos[3] = jnp.transpose(jnp.broadcast_to(mask, (N, N)))
    fe[0:N, :] = feat_ref[...]
    pf[...] = jnp.zeros_like(pf)
    back[...] = jnp.zeros_like(back)
    delta[CENTER] = jnp.zeros((4, N), F32)
    sp[...] = jnp.zeros_like(sp)
    vv[...] = jnp.zeros_like(vv)
    rt[...] = jnp.zeros_like(rt)
    def geometry(tile, rows):
        off_x = jnp.asarray((tile // 3 - 1) * 6, F32)
        off_y = jnp.asarray((tile % 3 - 1) * 6 if isinstance(tile, int) else (lax.rem(tile, 3) - 1) * 6, F32)
        part = pack[tile]
        disp = [
            (part[0:1] + off_x) - own_pos[0, rows, :],
            (part[1:2] + off_y) - own_pos[1, rows, :],
            part[2:3] - own_pos[2, rows, :],
        ]
        return part, disp

    def shape_tile(tile, spot, chunk):
        start = pl.multiple_of(chunk * ROWS, ROWS)
        rows = pl.ds(start, ROWS)
        cols = pl.ds(pl.multiple_of(spot * N, N), N)
        part, disp = geometry(tile, rows)
        scaled = (disp[0] * disp[0] + disp[1] * disp[1] + disp[2] * disp[2]) * (1.0 / 36.0)
        same = (lax.broadcasted_iota(jnp.int32, (ROWS, N), 0) + start) == lax.broadcasted_iota(jnp.int32, (ROWS, N), 1)
        centred = jnp.where(tile == CENTER, 1.0, 0.0)
        paired = own_pos[3, rows, :] * part[3:4] * (1.0 - jnp.where(same, 1.0, 0.0) * centred)
        margin = jnp.maximum(1.0 - scaled, 0.0)
        square = margin * margin * paired
        smooth = margin * square
        slope = -3.0 * square
        ang = [disp[b] * (1.0 / 6.0) for b in range(3)]
        for k in range(NB):
            decay = jnp.exp(scaled * (-RATES[k]))
            radial = decay * smooth
            phi[tile * NB + k, rows, :] = radial
            phis[tile * NB + k, rows, :] = decay * (slope - RATES[k] * smooth)
            for b in range(3):
                line = pl.ds(pl.multiple_of((k * 3 + b) * N + start, ROWS), ROWS)
                kb[line, cols] = (radial * ang[b]).astype(BF16)

    def own_shape(chunk, carry):
        shape_tile(jnp.int32(CENTER), 0, chunk)
        return carry

    lax.fori_loop(0, CHUNKS, own_shape, 0)
    pl.semaphore_wait(barrier, signals)

    def send_pack(tile):
        slot = TILES - 1 - tile
        return pltpu.make_async_remote_copy(
            src_ref=pack.at[CENTER], dst_ref=pack.at[slot], send_sem=send_pos.at[slot], recv_sem=recv_pos.at[slot],
            device_id=neighbour(tile), device_id_type=MESH)

    def send_features(source, tile, slot):
        block = feat_ref if source == CENTER else fe.at[pl.ds(PLACE[source] * N, N), :]
        return pltpu.make_async_remote_copy(
            src_ref=block, dst_ref=fe.at[pl.ds(PLACE[slot] * N, N), :], send_sem=send_feat.at[slot], recv_sem=recv_feat.at[slot],
            device_id=neighbour(tile), device_id_type=MESH)

    pack_copies = {t: send_pack(t) for t in around}
    for t in (0, 1, 2, 6, 7, 8, 3, 5):
        pack_copies[t].start()
    feat_copies = {7: send_features(CENTER, 1, 7), 1: send_features(CENTER, 7, 1),
                   5: send_features(CENTER, 3, 5), 3: send_features(CENTER, 5, 3)}
    for t in (7, 1, 5, 3):
        feat_copies[t].start()

    def shape_other(spot, power):
        tile = lax.rem(TABLE // power, 9)
        pltpu.make_async_remote_copy(
            src_ref=pack.at[CENTER], dst_ref=pack.at[tile], send_sem=send_pos.at[tile], recv_sem=recv_pos.at[tile],
            device_id=neighbour(0), device_id_type=MESH).wait_recv()

        def shape_rows(chunk, carry):
            shape_tile(tile, spot, chunk)
            return carry

        lax.fori_loop(0, CHUNKS, shape_rows, 0)
        return power * 9

    lax.fori_loop(1, TILES, shape_other, jnp.int32(9))

    def gather_part(first_col, last_col, mode):
        def gather_vectors(half, carry):
            first = pl.multiple_of(half * 768, 768)
            lines = pl.ds(first, 768)
            sums = jnp.dot(kb[lines, first_col:last_col], fe[first_col:last_col, :], preferred_element_type=F32)
            if mode > 0:
                sums = sums + ak[lines, :]
            ak[lines, :] = sums
            if mode == 2:
                vv[...] += sums[:384] * w_ref[pl.ds(half * 2, 1), :] + sums[384:] * w_ref[pl.ds(half * 2 + 1, 1), :]
            return carry

        lax.fori_loop(0, NB // 2, gather_vectors, 0)

    feat_copies[3].wait_recv()
    feat_copies[5].wait_recv()
    gather_part(0, 3 * N, 0)
    feat_copies[7].wait_recv()
    feat_copies[1].wait_recv()
    for source, tile in ((1, 3), (7, 3), (1, 5), (7, 5)):
        slot = source + (1 if tile == 3 else -1)
        feat_copies[slot] = send_features(source, tile, slot)
        feat_copies[slot].start()
    gather_part(3 * N, 5 * N, 1)
    for slot in (0, 2, 6, 8):
        feat_copies[slot].wait_recv()
    gather_part(5 * N, 9 * N, 2)

    lin_row = lin_ref[...].astype(BF16).astype(F32)
    high, low = split_rows(w_ref[...] * lin_row)
    cw[3072:3088, :] = jnp.concatenate([high, low], axis=0)
    pair_dims = (((1,), (1,)), ((), ()))
    twice = 2.0 * sq_ref[...]
    for k in range(NB):
        cw[k * 384 : (k + 1) * 384, :] = (vv[...] * (twice * w_ref[k : k + 1, :])).astype(BF16)

    def send_back_row(tile):
        return pltpu.make_async_remote_copy(
            src_ref=back.at[tile], dst_ref=back_in.at[tile], send_sem=send_back.at[tile], recv_sem=recv_back.at[tile],
            device_id=neighbour(tile), device_id_type=MESH)

    def pull_tile(step, power):
        spot = TILES - 1 - step
        tile = lax.rem(TABLE // power, 9)
        block = fe[pl.ds(pl.multiple_of(spot * N, N), N), :]
        ps[...] = lax.dot_general(cw[...], block, pair_dims, preferred_element_type=F32)
        level = ps[3072:3080, :] + ps[3080:3088, :]

        def pull_rows(chunk, totals):
            start = pl.multiple_of(chunk * ROWS, ROWS)
            rows = pl.ds(start, ROWS)
            part, disp = geometry(tile, rows)
            ang = [disp[b] * (1.0 / 6.0) for b in range(3)]
            along = jnp.zeros((ROWS, N), F32)
            across = [jnp.zeros((ROWS, N), F32) for _ in range(3)]
            for k in range(NB):
                radial = phi[tile * NB + k, rows, :]
                inner = level[k : k + 1, :]
                for b in range(3):
                    pair = ps[pl.ds(pl.multiple_of((k * 3 + b) * N + start, ROWS), ROWS), :]
                    inner = inner + ang[b] * pair
                    across[b] = across[b] + radial * pair
                along = along + phis[tile * NB + k, rows, :] * inner
            along = along * (1.0 / 3.0)
            sums = []
            for b in range(3):
                pull = along * ang[b] + across[b] * (1.0 / 6.0)
                pf[b, rows, :] += pull
                sums.append(totals[b] + fold(pull))
            return tuple(sums)

        zero = jnp.zeros((8, N), F32)
        totals = lax.fori_loop(0, CHUNKS, pull_rows, (zero, zero, zero))
        for b in range(3):
            back[tile, b : b + 1] = jnp.sum(totals[b], axis=0, keepdims=True)

        @pl.when(tile != CENTER)
        def _():
            send_back_row(tile).start()

        return power // 9

    lax.fori_loop(0, TILES, pull_tile, jnp.int32(9**8))
    forces = jnp.concatenate(
        [jnp.sum(jnp.transpose(pf[b]), axis=0, keepdims=True) for b in range(3)], axis=0) - back[CENTER, 0:3]
    for tile in around:
        send_back_row(tile).wait_recv()
        forces = forces - back_in[tile, 0:3]
    weights = conf_ref[...] * mask
    difference = forces - jnp.concatenate([teach_ref[b] for b in range(3)], axis=0)
    atom_total = 1.0 / float(nx * ny * N)
    for b in range(3):
        force_ref[b] = forces[b : b + 1]
    loss_row = jnp.sum(weights * difference * difference, axis=0, keepdims=True) * atom_total
    delta[CENTER, 0:3] = (-2.0 * atom_total) * weights * difference

    def send_error(tile):
        slot = TILES - 1 - tile
        return pltpu.make_async_remote_copy(
            src_ref=delta.at[CENTER], dst_ref=delta.at[slot], send_sem=send_delta.at[slot], recv_sem=recv_delta.at[slot],
            device_id=neighbour(tile), device_id_type=MESH)

    for t in (0, 1, 2, 6, 7, 8, 3, 5):
        send_error(t).start()
    for b in range(3):
        own_dir[b] = jnp.transpose(jnp.broadcast_to(delta[CENTER, b : b + 1], (N, N)))

    def move_tile(tile, spot, chunk):
        start = pl.multiple_of(chunk * ROWS, ROWS)
        rows = pl.ds(start, ROWS)
        cols = pl.ds(pl.multiple_of(spot * N, N), N)
        part, disp = geometry(tile, rows)
        ang = [disp[b] * (1.0 / 6.0) for b in range(3)]
        errors = delta[tile]
        turn = [(errors[b : b + 1] - own_dir[b, rows, :]) * (1.0 / 6.0) for b in range(3)]
        scaled_rate = 2.0 * (ang[0] * turn[0] + ang[1] * turn[1] + ang[2] * turn[2])
        for k in range(NB):
            level = phis[tile * NB + k, rows, :] * scaled_rate
            radial = phi[tile * NB + k, rows, :]
            sp[tile * NB + k] += fold(level)
            for b in range(3):
                line = pl.ds(pl.multiple_of((k * 3 + b) * N + start, ROWS), ROWS)
                kb[line, cols] = (level * ang[b] + radial * turn[b]).astype(BF16)

    def move_spot(spot, power):
        tile = lax.rem(TABLE // power, 9)

        @pl.when(spot > 0)
        def _():
            pltpu.make_async_remote_copy(
                src_ref=delta.at[CENTER], dst_ref=delta.at[tile], send_sem=send_delta.at[tile],
                recv_sem=recv_delta.at[tile], device_id=neighbour(0), device_id_type=MESH).wait_recv()

        def move_rows(chunk, carry):
            move_tile(tile, spot, chunk)
            return carry

        lax.fori_loop(0, CHUNKS, move_rows, 0)
        return power * 9

    lax.fori_loop(0, TILES, move_spot, jnp.int32(1))

    def gather_rates(half, carry):
        first = pl.multiple_of(half * 768, 768)
        sums = jnp.dot(kb[pl.ds(first, 768), :], fe[...], preferred_element_type=F32)
        rt[...] += sums[:384] * w_ref[pl.ds(half * 2, 1), :] + sums[384:] * w_ref[pl.ds(half * 2 + 1, 1), :]
        gp[half * 2] = fold(sums[:384] * vv[...])
        gp[half * 2 + 1] = fold(sums[384:] * vv[...])
        return carry

    lax.fori_loop(0, NB // 2, gather_rates, 0)

    def weigh(k, carry):
        lines = pl.ds(pl.multiple_of(k * 384, 384), 384)
        gp[k] += fold(ak[lines, :] * rt[...])
        return carry

    lax.fori_loop(0, NB, weigh, 0)
    level_sum = jnp.zeros((NB, N), F32)
    for t in range(TILES):
        high, low = split_rows(jnp.sum(sp[t * NB : (t + 1) * NB], axis=1))
        block = fe[PLACE[t] * N : (PLACE[t] + 1) * N, :]
        level_sum = level_sum + jnp.dot(high, block, preferred_element_type=F32) + jnp.dot(
            low, block, preferred_element_type=F32)
    result = jnp.concatenate([
        jnp.sum(gp[...], axis=1) * twice + lin_row * level_sum,
        2.0 * jnp.sum(fold(vv[...] * rt[...]), axis=0, keepdims=True),
        jnp.sum(w_ref[...] * level_sum, axis=0, keepdims=True),
        loss_row,
        jnp.zeros((G_ROWS - NB - 3, N), F32),
    ], axis=0)

    number = 0
    for group, buf in zip(groups, ar_bufs):
        place = member(group, 0)[0]
        buf[place] = result
        copies = []
        for step in range(1, size_of(group)):
            copy = pltpu.make_async_remote_copy(
                src_ref=buf.at[place], dst_ref=buf.at[place], send_sem=send_ar.at[number], recv_sem=recv_ar.at[number],
                device_id=member(group, step)[1], device_id_type=MESH)
            number += 1
            copy.start()
            copies.append(copy)
        for copy in copies:
            copy.wait_recv()
        result = jnp.sum(buf[...], axis=0)
        for copy in copies:
            copy.wait_send()

    sum_ref[...] = result
    for tile in around:
        pack_copies[tile].wait_send()
        feat_copies[tile].wait_send()
        send_back_row(tile).wait_send()
        send_error(tile).wait_send()


def finish(force_ref, sum_ref, out_ref, loss_ref, gw_ref, gsq_ref, glin_ref):
    out_ref[...] = force_ref[...]
    gw_ref[...] = sum_ref[0:NB]
    gsq_ref[...] = sum_ref[NB : NB + 1]
    glin_ref[...] = sum_ref[NB + 1 : NB + 2]
    loss_ref[...] = jnp.sum(sum_ref[NB + 2 : NB + 3], axis=1, keepdims=True)


def body(nx, ny, positions, features, counts, teacher, confidence, radial_weights, square_coef, linear_coef):
    groups = groups_of(nx, ny)
    copies = sum(size_of(g) - 1 for g in groups)
    vmem = pl.BlockSpec(memory_space=pltpu.VMEM)
    forces, sums = pl.pallas_call(
        functools.partial(kernel, nx, ny),
        out_shape=(jax.ShapeDtypeStruct((3, 1, N), F32), jax.ShapeDtypeStruct((G_ROWS, N), F32)),
        in_specs=[vmem] * 8,
        out_specs=(vmem,) * 2,
        scratch_shapes=[
            pltpu.VMEM((TILES, 4, N), F32),
            pltpu.VMEM((TILES * N, N), BF16),
            pltpu.VMEM((4, N, N), F32),
            pltpu.VMEM((TILES * NB, N, N), F32),
            pltpu.VMEM((TILES * NB, N, N), F32),
            pltpu.VMEM((3 * NB * N, TILES * N), BF16),
            pltpu.VMEM((3 * NB * N, N), F32),
            pltpu.VMEM((3 * N, N), F32),
            pltpu.VMEM((3 * NB * N + 16, N), BF16),
            pltpu.VMEM((3 * NB * N + 16, N), F32),
            pltpu.VMEM((3, N, N), F32),
            pltpu.VMEM((TILES, 4, N), F32),
            pltpu.VMEM((TILES, 4, N), F32),
            pltpu.VMEM((TILES, 4, N), F32),
            pltpu.VMEM((3, N, N), F32),
            pltpu.VMEM((TILES * NB, 8, N), F32),
            pltpu.VMEM((3 * N, N), F32),
            pltpu.VMEM((NB, 8, N), F32),
        ]
        + [pltpu.VMEM((size_of(g), G_ROWS, N), F32) for g in groups]
        + [pltpu.SemaphoreType.DMA((TILES,))] * 8
        + [pltpu.SemaphoreType.DMA((copies,))] * 2,
        compiler_params=pltpu.CompilerParams(
            collective_id=0, has_side_effects=True, vmem_limit_bytes=60 * 1024 * 1024),
        name="message_layer",
    )(
        positions.reshape(3, 1, N), features.reshape(N, N), counts, teacher.reshape(3, 1, N), confidence.reshape(1, N),
        radial_weights, square_coef.reshape(1, N), linear_coef.reshape(1, N),
    )
    forces, loss, grad_w, grad_sq, grad_lin = pl.pallas_call(
        finish,
        out_shape=(
            jax.ShapeDtypeStruct((3, 1, N), F32),
            jax.ShapeDtypeStruct((1, 1), F32),
            jax.ShapeDtypeStruct((NB, N), F32),
            jax.ShapeDtypeStruct((1, N), F32),
            jax.ShapeDtypeStruct((1, N), F32),
        ),
        in_specs=[vmem] * 2,
        out_specs=(vmem,) * 5,
        name="finish",
    )(forces, sums)
    return (forces.reshape(1, 1, 3, N), loss.reshape(()), grad_w, grad_sq.reshape(N), grad_lin.reshape(N))


def solution(mesh):
    in_specs = (
        P("gx", "gy", None, None),
        P("gx", "gy", None, None),
        P("gx", "gy"),
        P("gx", "gy", None, None),
        P("gx", "gy", None),
        P(),
        P(),
        P(),
    )
    out_specs = (P("gx", "gy", None, None), P(), P(), P(), P())
    step = functools.partial(body, mesh.shape["gx"], mesh.shape["gy"])
    return jax.shard_map(step, mesh=mesh, in_specs=in_specs, out_specs=out_specs, check_vma=False)
```

```python
import functools

import numpy as np
import jax
import jax.numpy as jnp
from jax import lax
from jax.experimental import pallas as pl
from jax.experimental.pallas import tpu as pltpu
from jax.sharding import PartitionSpec as P

EDGE = 6.0
MESH = pl.DeviceIdType.MESH
F32 = jnp.float32
BF16 = jnp.bfloat16
N = 128
NB = 8
TILES = 9
CENTER = 4
ROWS = 32
PULL_ROWS = 8
CHUNKS = N // ROWS
RATES = [float(np.float32(0.5) * np.float32(1.6) ** np.float32(k)) for k in range(NB)]
G_ROWS = 12
ORDER = (4, 3, 5, 1, 7, 0, 2, 6, 8)
PLACE = tuple(ORDER.index(t) for t in range(TILES))
TABLE = sum(t * 9**p for p, t in enumerate(ORDER))


def shift_of(tile):
    return tile // 3 - 1, tile % 3 - 1


def groups_of(nx, ny):
    inner_y = min(8, ny)
    inner_x = min(4, nx)
    groups = [
        (("gy", 1, inner_y),),
        (("gx", inner_x, nx // inner_x), ("gy", inner_y, ny // inner_y)),
        (("gx", 1, inner_x),),
    ]
    return [g for g in groups if size_of(g) > 1]


def size_of(group):
    total = 1
    for part in group:
        total *= part[2]
    return total


def fold(values):
    rows, cols = values.shape
    return jnp.sum(values.reshape(rows // 8, 8, cols), axis=0)


def split_rows(values):
    high = values.astype(BF16)
    low = (values - high.astype(F32)).astype(BF16)
    return high, low


def kernel(
    nx, ny, pos_ref, feat_ref, count_ref, teach_ref, conf_ref, w_ref, sq_ref, lin_ref,
    force_ref, sum_ref,
    pack, fe, own_pos, phi, phis, kb, ak, vv, cw, ps_a, ps_b, pf, back, back_in, delta, own_dir, sp, rt, gp, *rest,
):
    groups = groups_of(nx, ny)
    ar_bufs = rest[: len(groups)]
    send_pos, recv_pos, send_feat, recv_feat, send_back, recv_back, send_delta, recv_delta, send_ar, recv_ar = rest[len(groups):]
    my_x = lax.axis_index("gx")
    my_y = lax.axis_index("gy")

    def neighbour(tile):
        off_x, off_y = shift_of(tile)
        return (lax.rem(my_x + off_x + nx, nx), lax.rem(my_y + off_y + ny, ny))

    def member(group, step):
        place = 0
        target = {"gx": my_x, "gy": my_y}
        for axis, stride, size in reversed(group):
            base = target[axis]
            spot = lax.rem(base // stride, size)
            place = place * size + spot
            target[axis] = base + (lax.rem(spot + step % size, size) - spot) * stride
            step = step // size
        return place, (target["gx"], target["gy"])

    around = [t for t in range(TILES) if t != CENTER]
    barrier = pltpu.get_barrier_semaphore()
    signals = 0
    for tile in around:
        pl.semaphore_signal(barrier, inc=1, device_id=neighbour(tile), device_id_type=MESH)
        signals += 1
    for group in groups:
        for step in range(1, size_of(group)):
            pl.semaphore_signal(barrier, inc=1, device_id=member(group, step)[1], device_id_type=MESH)
            signals += 1

    mask = (lax.broadcasted_iota(jnp.int32, (1, N), 1) < count_ref[...]).astype(F32)
    for b in range(3):
        pack[CENTER, b : b + 1] = pos_ref[b]
    pack[CENTER, 3:4] = mask
    for b in range(3):
        own_pos[b] = jnp.transpose(jnp.broadcast_to(pos_ref[b], (N, N)))
    own_pos[3] = jnp.transpose(jnp.broadcast_to(mask, (N, N)))
    fe[0:N, :] = feat_ref[...]
    pf[...] = jnp.zeros_like(pf)
    back[...] = jnp.zeros_like(back)
    delta[CENTER] = jnp.zeros((4, N), F32)
    sp[...] = jnp.zeros_like(sp)
    vv[...] = jnp.zeros_like(vv)
    rt[...] = jnp.zeros_like(rt)
    def geometry(tile, rows):
        off_x = jnp.asarray((tile // 3 - 1) * 6, F32)
        off_y = jnp.asarray((tile % 3 - 1) * 6 if isinstance(tile, int) else (lax.rem(tile, 3) - 1) * 6, F32)
        part = pack[tile]
        disp = [
            (part[0:1] + off_x) - own_pos[0, rows, :],
            (part[1:2] + off_y) - own_pos[1, rows, :],
            part[2:3] - own_pos[2, rows, :],
        ]
        return part, disp

    def shape_tile(tile, spot, chunk):
        start = pl.multiple_of(chunk * ROWS, ROWS)
        rows = pl.ds(start, ROWS)
        cols = pl.ds(pl.multiple_of(spot * N, N), N)
        part, disp = geometry(tile, rows)
        scaled = (disp[0] * disp[0] + disp[1] * disp[1] + disp[2] * disp[2]) * (1.0 / 36.0)
        same = (lax.broadcasted_iota(jnp.int32, (ROWS, N), 0) + start) == lax.broadcasted_iota(jnp.int32, (ROWS, N), 1)
        centred = jnp.where(tile == CENTER, 1.0, 0.0)
        paired = own_pos[3, rows, :] * part[3:4] * (1.0 - jnp.where(same, 1.0, 0.0) * centred)
        margin = jnp.maximum(1.0 - scaled, 0.0)
        square = margin * margin * paired
        smooth = margin * square
        slope = -3.0 * square
        ang = [disp[b] * (1.0 / 6.0) for b in range(3)]
        for k in range(NB):
            decay = jnp.exp(scaled * (-RATES[k]))
            radial = decay * smooth
            phi[tile * NB + k, rows, :] = radial
            phis[tile * NB + k, rows, :] = decay * (slope - RATES[k] * smooth)
            for b in range(3):
                line = pl.ds(pl.multiple_of((k * 3 + b) * N + start, ROWS), ROWS)
                kb[line, cols] = (radial * ang[b]).astype(BF16)

    def own_shape(chunk, carry):
        shape_tile(jnp.int32(CENTER), 0, chunk)
        return carry

    lax.fori_loop(0, CHUNKS, own_shape, 0)
    pl.semaphore_wait(barrier, signals)

    def send_pack(tile):
        slot = TILES - 1 - tile
        return pltpu.make_async_remote_copy(
            src_ref=pack.at[CENTER], dst_ref=pack.at[slot], send_sem=send_pos.at[slot], recv_sem=recv_pos.at[slot],
            device_id=neighbour(tile), device_id_type=MESH)

    def send_features(source, tile, slot):
        block = feat_ref if source == CENTER else fe.at[pl.ds(PLACE[source] * N, N), :]
        return pltpu.make_async_remote_copy(
            src_ref=block, dst_ref=fe.at[pl.ds(PLACE[slot] * N, N), :], send_sem=send_feat.at[slot], recv_sem=recv_feat.at[slot],
            device_id=neighbour(tile), device_id_type=MESH)

    pack_copies = {t: send_pack(t) for t in around}
    for t in (0, 1, 2, 6, 7, 8, 3, 5):
        pack_copies[t].start()
    feat_copies = {7: send_features(CENTER, 1, 7), 1: send_features(CENTER, 7, 1),
                   5: send_features(CENTER, 3, 5), 3: send_features(CENTER, 5, 3)}
    for t in (7, 1, 5, 3):
        feat_copies[t].start()

    def shape_other(spot, power):
        tile = lax.rem(TABLE // power, 9)
        pltpu.make_async_remote_copy(
            src_ref=pack.at[CENTER], dst_ref=pack.at[tile], send_sem=send_pos.at[tile], recv_sem=recv_pos.at[tile],
            device_id=neighbour(0), device_id_type=MESH).wait_recv()

        def shape_rows(chunk, carry):
            shape_tile(tile, spot, chunk)
            return carry

        lax.fori_loop(0, CHUNKS, shape_rows, 0)
        return power * 9

    lax.fori_loop(1, TILES, shape_other, jnp.int32(9))

    def gather_part(first_col, last_col, mode):
        def gather_vectors(half, carry):
            first = pl.multiple_of(half * 768, 768)
            lines = pl.ds(first, 768)
            sums = jnp.dot(kb[lines, first_col:last_col], fe[first_col:last_col, :], preferred_element_type=F32)
            if mode > 0:
                sums = sums + ak[lines, :]
            ak[lines, :] = sums
            if mode == 2:
                vv[...] += sums[:384] * w_ref[pl.ds(half * 2, 1), :] + sums[384:] * w_ref[pl.ds(half * 2 + 1, 1), :]
            return carry

        lax.fori_loop(0, NB // 2, gather_vectors, 0)

    feat_copies[3].wait_recv()
    feat_copies[5].wait_recv()
    gather_part(0, 3 * N, 0)
    feat_copies[7].wait_recv()
    feat_copies[1].wait_recv()
    for source, tile in ((1, 3), (7, 3), (1, 5), (7, 5)):
        slot = source + (1 if tile == 3 else -1)
        feat_copies[slot] = send_features(source, tile, slot)
        feat_copies[slot].start()
    gather_part(3 * N, 5 * N, 1)
    for slot in (0, 2, 6, 8):
        feat_copies[slot].wait_recv()
    gather_part(5 * N, 9 * N, 2)

    lin_row = lin_ref[...].astype(BF16).astype(F32)
    high, low = split_rows(w_ref[...] * lin_row)
    cw[3072:3088, :] = jnp.concatenate([high, low], axis=0)
    pair_dims = (((1,), (1,)), ((), ()))
    twice = 2.0 * sq_ref[...]
    for k in range(NB):
        cw[k * 384 : (k + 1) * 384, :] = (vv[...] * (twice * w_ref[k : k + 1, :])).astype(BF16)

    def send_back_row(tile):
        return pltpu.make_async_remote_copy(
            src_ref=back.at[tile], dst_ref=back_in.at[tile], send_sem=send_back.at[tile], recv_sem=recv_back.at[tile],
            device_id=neighbour(tile), device_id_type=MESH)

    def pair_spot(spot, ps):
        block = fe[pl.ds(pl.multiple_of(spot * N, N), N), :]
        ps[...] = lax.dot_general(cw[...], block, pair_dims, preferred_element_type=F32)

    def pull_tile(tile, ps):
        level = ps[3072:3080, :] + ps[3080:3088, :]
        totals = [jnp.zeros((8, N), F32) for _ in range(3)]
        for chunk in range(N // PULL_ROWS):
            start = chunk * PULL_ROWS
            rows = slice(start, start + PULL_ROWS)
            part, disp = geometry(tile, rows)
            ang = [disp[b] * (1.0 / 6.0) for b in range(3)]
            along = jnp.zeros((PULL_ROWS, N), F32)
            across = [jnp.zeros((PULL_ROWS, N), F32) for _ in range(3)]
            for k in range(NB):
                radial = phi[tile * NB + k, rows, :]
                inner = level[k : k + 1, :]
                for b in range(3):
                    first = (k * 3 + b) * N + start
                    pair = ps[first : first + PULL_ROWS, :]
                    inner = inner + ang[b] * pair
                    across[b] = across[b] + radial * pair
                along = along + phis[tile * NB + k, rows, :] * inner
            along = along * (1.0 / 3.0)
            for b in range(3):
                pull = along * ang[b] + across[b] * (1.0 / 6.0)
                pf[b, rows, :] += pull
                totals[b] = totals[b] + fold(pull)
        for b in range(3):
            back[tile, b : b + 1] = jnp.sum(totals[b], axis=0, keepdims=True)

    def pull_two(step, power):
        spot = TILES - 1 - 2 * step
        tile = lax.rem(TABLE // power, 9)
        pair_spot(spot - 1, ps_b)
        pull_tile(tile, ps_a)
        send_back_row(tile).start()
        tile = lax.rem(TABLE // (power // 9), 9)
        pair_spot(spot - 2, ps_a)
        pull_tile(tile, ps_b)
        send_back_row(tile).start()
        return power // 81

    pair_spot(TILES - 1, ps_a)
    lax.fori_loop(0, TILES // 2, pull_two, jnp.int32(9**8))
    pull_tile(jnp.int32(CENTER), ps_a)
    forces = jnp.concatenate(
        [jnp.sum(jnp.transpose(pf[b]), axis=0, keepdims=True) for b in range(3)], axis=0) - back[CENTER, 0:3]
    for tile in around:
        send_back_row(tile).wait_recv()
        forces = forces - back_in[tile, 0:3]
    weights = conf_ref[...] * mask
    difference = forces - jnp.concatenate([teach_ref[b] for b in range(3)], axis=0)
    atom_total = 1.0 / float(nx * ny * N)
    for b in range(3):
        force_ref[b] = forces[b : b + 1]
    loss_row = jnp.sum(weights * difference * difference, axis=0, keepdims=True) * atom_total
    delta[CENTER, 0:3] = (-2.0 * atom_total) * weights * difference

    def send_error(tile):
        slot = TILES - 1 - tile
        return pltpu.make_async_remote_copy(
            src_ref=delta.at[CENTER], dst_ref=delta.at[slot], send_sem=send_delta.at[slot], recv_sem=recv_delta.at[slot],
            device_id=neighbour(tile), device_id_type=MESH)

    for t in (0, 1, 2, 6, 7, 8, 3, 5):
        send_error(t).start()
    for b in range(3):
        own_dir[b] = jnp.transpose(jnp.broadcast_to(delta[CENTER, b : b + 1], (N, N)))

    def move_tile(tile, spot, chunk):
        start = pl.multiple_of(chunk * ROWS, ROWS)
        rows = pl.ds(start, ROWS)
        cols = pl.ds(pl.multiple_of(spot * N, N), N)
        part, disp = geometry(tile, rows)
        ang = [disp[b] * (1.0 / 6.0) for b in range(3)]
        errors = delta[tile]
        turn = [(errors[b : b + 1] - own_dir[b, rows, :]) * (1.0 / 6.0) for b in range(3)]
        scaled_rate = 2.0 * (ang[0] * turn[0] + ang[1] * turn[1] + ang[2] * turn[2])
        for k in range(NB):
            level = phis[tile * NB + k, rows, :] * scaled_rate
            radial = phi[tile * NB + k, rows, :]
            sp[tile * NB + k] += fold(level)
            for b in range(3):
                line = pl.ds(pl.multiple_of((k * 3 + b) * N + start, ROWS), ROWS)
                kb[line, cols] = (level * ang[b] + radial * turn[b]).astype(BF16)

    def move_spot(spot, power):
        tile = lax.rem(TABLE // power, 9)

        @pl.when(spot > 0)
        def _():
            pltpu.make_async_remote_copy(
                src_ref=delta.at[CENTER], dst_ref=delta.at[tile], send_sem=send_delta.at[tile],
                recv_sem=recv_delta.at[tile], device_id=neighbour(0), device_id_type=MESH).wait_recv()

        def move_rows(chunk, carry):
            move_tile(tile, spot, chunk)
            return carry

        lax.fori_loop(0, CHUNKS, move_rows, 0)
        return power * 9

    lax.fori_loop(0, TILES, move_spot, jnp.int32(1))

    def gather_rates(half, carry):
        first = pl.multiple_of(half * 768, 768)
        sums = jnp.dot(kb[pl.ds(first, 768), :], fe[...], preferred_element_type=F32)
        rt[...] += sums[:384] * w_ref[pl.ds(half * 2, 1), :] + sums[384:] * w_ref[pl.ds(half * 2 + 1, 1), :]
        gp[half * 2] = fold(sums[:384] * vv[...])
        gp[half * 2 + 1] = fold(sums[384:] * vv[...])
        return carry

    lax.fori_loop(0, NB // 2, gather_rates, 0)

    def weigh(k, carry):
        lines = pl.ds(pl.multiple_of(k * 384, 384), 384)
        gp[k] += fold(ak[lines, :] * rt[...])
        return carry

    lax.fori_loop(0, NB, weigh, 0)
    level_sum = jnp.zeros((NB, N), F32)
    for t in range(TILES):
        high, low = split_rows(jnp.sum(sp[t * NB : (t + 1) * NB], axis=1))
        block = fe[PLACE[t] * N : (PLACE[t] + 1) * N, :]
        level_sum = level_sum + jnp.dot(high, block, preferred_element_type=F32) + jnp.dot(
            low, block, preferred_element_type=F32)
    result = jnp.concatenate([
        jnp.sum(gp[...], axis=1) * twice + lin_row * level_sum,
        2.0 * jnp.sum(fold(vv[...] * rt[...]), axis=0, keepdims=True),
        jnp.sum(w_ref[...] * level_sum, axis=0, keepdims=True),
        loss_row,
        jnp.zeros((G_ROWS - NB - 3, N), F32),
    ], axis=0)

    number = 0
    for group, buf in zip(groups, ar_bufs):
        place = member(group, 0)[0]
        buf[place] = result
        copies = []
        for step in range(1, size_of(group)):
            copy = pltpu.make_async_remote_copy(
                src_ref=buf.at[place], dst_ref=buf.at[place], send_sem=send_ar.at[number], recv_sem=recv_ar.at[number],
                device_id=member(group, step)[1], device_id_type=MESH)
            number += 1
            copy.start()
            copies.append(copy)
        for copy in copies:
            copy.wait_recv()
        result = jnp.sum(buf[...], axis=0)
        for copy in copies:
            copy.wait_send()

    sum_ref[...] = result
    for tile in around:
        pack_copies[tile].wait_send()
        feat_copies[tile].wait_send()
        send_back_row(tile).wait_send()
        send_error(tile).wait_send()


def finish(force_ref, sum_ref, out_ref, loss_ref, gw_ref, gsq_ref, glin_ref):
    out_ref[...] = force_ref[...]
    gw_ref[...] = sum_ref[0:NB]
    gsq_ref[...] = sum_ref[NB : NB + 1]
    glin_ref[...] = sum_ref[NB + 1 : NB + 2]
    loss_ref[...] = jnp.sum(sum_ref[NB + 2 : NB + 3], axis=1, keepdims=True)


def body(nx, ny, positions, features, counts, teacher, confidence, radial_weights, square_coef, linear_coef):
    groups = groups_of(nx, ny)
    copies = sum(size_of(g) - 1 for g in groups)
    vmem = pl.BlockSpec(memory_space=pltpu.VMEM)
    forces, sums = pl.pallas_call(
        functools.partial(kernel, nx, ny),
        out_shape=(jax.ShapeDtypeStruct((3, 1, N), F32), jax.ShapeDtypeStruct((G_ROWS, N), F32)),
        in_specs=[vmem] * 8,
        out_specs=(vmem,) * 2,
        scratch_shapes=[
            pltpu.VMEM((TILES, 4, N), F32),
            pltpu.VMEM((TILES * N, N), BF16),
            pltpu.VMEM((4, N, N), F32),
            pltpu.VMEM((TILES * NB, N, N), F32),
            pltpu.VMEM((TILES * NB, N, N), F32),
            pltpu.VMEM((3 * NB * N, TILES * N), BF16),
            pltpu.VMEM((3 * NB * N, N), F32),
            pltpu.VMEM((3 * N, N), F32),
            pltpu.VMEM((3 * NB * N + 16, N), BF16),
            pltpu.VMEM((3 * NB * N + 16, N), F32),
            pltpu.VMEM((3 * NB * N + 16, N), F32),
            pltpu.VMEM((3, N, N), F32),
            pltpu.VMEM((TILES, 4, N), F32),
            pltpu.VMEM((TILES, 4, N), F32),
            pltpu.VMEM((TILES, 4, N), F32),
            pltpu.VMEM((3, N, N), F32),
            pltpu.VMEM((TILES * NB, 8, N), F32),
            pltpu.VMEM((3 * N, N), F32),
            pltpu.VMEM((NB, 8, N), F32),
        ]
        + [pltpu.VMEM((size_of(g), G_ROWS, N), F32) for g in groups]
        + [pltpu.SemaphoreType.DMA((TILES,))] * 8
        + [pltpu.SemaphoreType.DMA((copies,))] * 2,
        compiler_params=pltpu.CompilerParams(
            collective_id=0, has_side_effects=True, vmem_limit_bytes=60 * 1024 * 1024),
        name="message_layer",
    )(
        positions.reshape(3, 1, N), features.reshape(N, N), counts, teacher.reshape(3, 1, N), confidence.reshape(1, N),
        radial_weights, square_coef.reshape(1, N), linear_coef.reshape(1, N),
    )
    forces, loss, grad_w, grad_sq, grad_lin = pl.pallas_call(
        finish,
        out_shape=(
            jax.ShapeDtypeStruct((3, 1, N), F32),
            jax.ShapeDtypeStruct((1, 1), F32),
            jax.ShapeDtypeStruct((NB, N), F32),
            jax.ShapeDtypeStruct((1, N), F32),
            jax.ShapeDtypeStruct((1, N), F32),
        ),
        in_specs=[vmem] * 2,
        out_specs=(vmem,) * 5,
        name="finish",
    )(forces, sums)
    return (forces.reshape(1, 1, 3, N), loss.reshape(()), grad_w, grad_sq.reshape(N), grad_lin.reshape(N))


def solution(mesh):
    in_specs = (
        P("gx", "gy", None, None),
        P("gx", "gy", None, None),
        P("gx", "gy"),
        P("gx", "gy", None, None),
        P("gx", "gy", None),
        P(),
        P(),
        P(),
    )
    out_specs = (P("gx", "gy", None, None), P(), P(), P(), P())
    step = functools.partial(body, mesh.shape["gx"], mesh.shape["gy"])
    return jax.shard_map(step, mesh=mesh, in_specs=in_specs, out_specs=out_specs, check_vma=False)
```
